32 devices in a mesh: sec: 4 (over y, x), dev: 8 (over z, core).
Axes of the slice: x: 2, y: 2, z: 4, core: 2. Of those that a mesh axis runs over, the one named last changes fastest.
Arguments:
- child_panel: bfloat16 [4, 6144, 2048], P('sec', 'dev'), may hold values from -0.23925781 to 0.23925781
- child_inverse: bfloat16 [4, 2048, 2048], P('sec'), may hold values from -0.03756505 to 1.5, as said below
- child_map: int32 [4, 48], replicated, may hold values from 0 to 63, as said below
- parent_front: bfloat16 [8192, 8192], P('sec', 'dev'), may hold values from -6 to 6
- parent_inverse: bfloat16 [1024, 1024], replicated, may hold values from -0.00166015625 to 0.046875, as said below
- parent_pivots: int32 [8], replicated, may hold values from 0 to 63, as said below
Outputs:
- parent_update: float32 [8192, 8192], P('sec', 'dev')
- parent_factor: bfloat16 [8192, 1024], P('sec')
The draws below stay inside these ranges and needn't reach their ends.
Inputs may be any that keep to these rules, and one draw needn't show every extreme that they name: `child_map`: each row names 48 different parent blocks. `parent_pivots`: 8 different parent blocks. `child_inverse`: upper triangular with positive diagonal. `parent_inverse`: upper triangular with positive diagonal.
All inputs are finite; a program needn't handle non-finite values.
Results may differ from the reference program's by a relative error of at most 0.014.
Values may be sent and summed in bfloat16 or wider, within the bound.
A program may use at most 128 MiB of HBM per device.

```python
import jax
import jax.numpy as jnp
from jax import lax

BLK = 128
PIV = 2048
CROWS = 6144
PORD = 8192
KP = 1024
CBLK = 48
PBLK = 64
KB = 8
N_SEC = 4


def upper_factor(key, order, diag_scale, off_scale):
    key_off, key_diag = jax.random.split(key, 2)
    off_part = jax.random.uniform(key_off, (order, order), jnp.float32, -1.6, 1.6) * off_scale
    diagonal = jax.random.uniform(key_diag, (order,), jnp.float32, 0.5, 1.45) * diag_scale
    return jnp.triu(off_part, 1) + jnp.diag(diagonal)


def spanning(key, count, total):
    key_rest, key_order = jax.random.split(key)
    middle = jax.random.permutation(key_rest, jnp.arange(1, total - 1, dtype=jnp.int32))[:count - 2]
    chosen = jnp.concatenate([jnp.array([0, total - 1], jnp.int32), middle])
    return jax.random.permutation(key_order, chosen)


def draw_child_inverse(key, part):
    keys = jax.random.split(jax.random.fold_in(key, 11), N_SEC)
    stacked = jax.vmap(lambda one_key: upper_factor(one_key, PIV, 1.0, PIV ** (-0.5)))(keys)
    return stacked.astype(jnp.bfloat16)


def draw_parent_inverse(key, part):
    return upper_factor(jax.random.fold_in(key, 13), KP, KP ** (-0.5), 1.0 / KP).astype(jnp.bfloat16)


def draw_child_map(key, part):
    keys = jax.random.split(jax.random.fold_in(key, 17), N_SEC)
    return jax.vmap(lambda one_key: spanning(one_key, CBLK, PBLK))(keys)


def draw_parent_pivots(key, part):
    return spanning(jax.random.fold_in(key, 19), KB, PBLK)


def block_scale(rng, extent, shards, smallest, largest):
    def one(dim, blocks):
        draws = jax.random.uniform(jax.random.fold_in(jax.random.fold_in(rng, 6), dim), (blocks,), jnp.float32, smallest / len(shards), largest / len(shards))
        return jnp.repeat(jnp.exp(draws), extent[dim] // blocks).reshape((-1,) + (1,) * (len(extent) - dim - 1))

    loudness = one(*shards[0])
    for cut in shards[1:]:
        loudness = loudness * one(*cut)
    return loudness


def gaussian(stream_key, dims, spread, most, shards=(), held_as=jnp.bfloat16):
    values = jax.random.normal(stream_key, dims, jnp.float32) * spread
    if len(shards) > 0:
        values = block_scale(stream_key, dims, shards, -0.22, 0.18) * values
    return jnp.clip(values, min=-most, max=most).astype(held_as)


def setup_inputs(seed: int = 0) -> dict:
    arg_keys = jax.random.split(jax.random.key(seed), 7)
    return {
        "child_panel": gaussian(arg_keys[0], (N_SEC, CROWS, PIV), 0.04, 0.23925781, ((0, 4), (1, 8))),
        "child_inverse": draw_child_inverse(jax.random.fold_in(arg_keys[6], 71), 0),
        "child_map": draw_child_map(jax.random.fold_in(arg_keys[6], 71), 0),
        "parent_front": gaussian(arg_keys[3], (PORD, PORD), 1.0, 6.0, ((0, 4), (1, 8))),
        "parent_inverse": draw_parent_inverse(jax.random.fold_in(arg_keys[6], 71), 0),
        "parent_pivots": draw_parent_pivots(jax.random.fold_in(arg_keys[6], 71), 0),
    }


def block_positions(blocks):
    offsets = jnp.arange(BLK, dtype=jnp.int32)
    return (blocks.astype(jnp.int32)[:, None] * BLK + offsets[None, :]).reshape(-1).astype(jnp.int32)


def product(left, right):
    return jnp.dot(left.astype(jnp.float32), right.astype(jnp.float32), precision=lax.Precision.HIGHEST)


def outer_rows(left_rows, right_rows):
    return lax.dot_general(left_rows.astype(jnp.float32), right_rows.astype(jnp.float32), (((1,), (1,)), ((), ())), precision=lax.Precision.HIGHEST)


def reference(child_panel, child_inverse, child_map, parent_front, parent_inverse, parent_pivots):
    summed_blocks = jnp.zeros((PBLK, BLK, PBLK, BLK), jnp.float32)
    for child_index in range(N_SEC):
        factor_rows = product(child_panel[child_index], child_inverse[child_index]).astype(jnp.bfloat16)
        contribution = (-outer_rows(factor_rows, factor_rows)).astype(jnp.bfloat16)
        pieces = contribution.astype(jnp.float32).reshape(CBLK, BLK, CBLK, BLK).transpose(0, 2, 1, 3)
        blocks = child_map[child_index].astype(jnp.int32)
        summed_blocks = summed_blocks.at[blocks[:, None], :, blocks[None, :], :].add(pieces)
    summed = summed_blocks.reshape(PORD, PORD)
    assembled = parent_front.astype(jnp.float32) + summed
    pivot_cols = block_positions(parent_pivots)
    panel_values = assembled[:, pivot_cols].astype(jnp.bfloat16)
    parent_factor = product(panel_values, parent_inverse).astype(jnp.bfloat16)
    is_pivot = jnp.zeros((PORD,), jnp.bool_).at[pivot_cols].set(True)
    trailing = jnp.where(is_pivot[:, None], jnp.zeros_like(parent_factor), parent_factor)
    parent_update = assembled - outer_rows(trailing, trailing)
    return parent_update, parent_factor
```

```python
import jax
import jax.numpy as jnp
from jax import lax
from jax.experimental import pallas as pl
from jax.experimental.pallas import tpu as pltpu
from jax.sharding import PartitionSpec as P

BLK = 128
PORD = 8192


GROUP = 4


def broadcast_rows(value, bits, dev_count, sec_count, roots, relative):
    reached = [0]
    for bit in bits:
        pairs = [
            ((roots[dev] ^ rel) * dev_count + dev, (roots[dev] ^ rel ^ bit) * dev_count + dev)
            for dev in range(dev_count)
            for rel in reached
        ]
        received = lax.ppermute(value, ("sec", "dev"), pairs)
        value = jnp.where((relative & bit) != 0, received, value)
        reached = reached + [rel ^ bit for rel in reached]
    return value


def placed_product(whole_rows, row_from, row_has, col_from, col_has):
    depth = whole_rows.shape[1]
    rows, cols = row_from.shape[0], col_from.shape[0]

    def kernel(row_from, row_has, col_from, col_has, *refs):
        left, right = refs[:GROUP], refs[GROUP:GROUP + cols]
        out, held = refs[GROUP + cols], refs[GROUP + cols + 1]
        step = pl.program_id(0)

        @pl.when(step == 0)
        def _():
            for k in range(cols):

                @pl.when(col_has[k] > 0)
                def _():
                    held[k * BLK:(k + 1) * BLK, :] = right[k][...]

                @pl.when(col_has[k] == 0)
                def _():
                    held[k * BLK:(k + 1) * BLK, :] = jnp.zeros((BLK, depth), held.dtype)

        product = outer_rows(jnp.concatenate([r[...] for r in left], axis=0), held[...])
        for k in range(GROUP):
            part = product[k * BLK:(k + 1) * BLK, :]
            kept = jnp.where(row_has[step * GROUP + k] > 0, -part, 0.0)
            out[k * BLK:(k + 1) * BLK, :] = kept.astype(out.dtype)

    def left_spec(k):
        return pl.BlockSpec((BLK, depth), lambda i, rf, rh, cf, ch: (rf[i * GROUP + k], 0))

    def right_spec(k):
        return pl.BlockSpec((BLK, depth), lambda i, rf, rh, cf, ch: (cf[k], 0))

    return pl.pallas_call(
        kernel,
        out_shape=jax.ShapeDtypeStruct((rows * BLK, cols * BLK), jnp.bfloat16),
        grid_spec=pltpu.PrefetchScalarGridSpec(
            num_scalar_prefetch=4,
            grid=(rows // GROUP,),
            in_specs=[left_spec(k) for k in range(GROUP)] + [right_spec(k) for k in range(cols)],
            out_specs=pl.BlockSpec((GROUP * BLK, cols * BLK), lambda i, rf, rh, cf, ch: (i, 0)),
            scratch_shapes=[pltpu.VMEM((cols * BLK, depth), jnp.bfloat16)],
        ),
        cost_estimate=pl.CostEstimate(
            flops=2 * rows * BLK * cols * BLK * depth,
            bytes_accessed=2 * rows * BLK * (depth + cols * BLK),
            transcendentals=0,
        ),
    )(row_from, row_has, col_from, col_has, *([whole_rows] * (GROUP + cols)))


def outer_rows(left_rows, right_rows):
    return lax.dot_general(
        left_rows, right_rows, (((1,), (1,)), ((), ())), preferred_element_type=jnp.float32
    )


def local(child_panel, child_inverse, child_map, parent_front, parent_inverse, parent_pivots):
    dev_count = lax.axis_size("dev")
    sec_count = lax.axis_size("sec")
    sec_index = lax.axis_index("sec")
    dev_index = lax.axis_index("dev")
    block_count = PORD // BLK
    cols_dev = block_count // dev_count
    rows_sec = block_count // sec_count
    col_width = cols_dev * BLK
    my_map = lax.dynamic_index_in_dim(child_map, sec_index, 0, keepdims=False)
    is_target = my_map[None, :] == jnp.arange(block_count, dtype=jnp.int32)[:, None]
    row_from = jnp.argmax(is_target, axis=1).astype(jnp.int32)
    row_has = jnp.any(is_target, axis=1).astype(jnp.int32)
    lower_rows = jnp.dot(
        child_panel[0], child_inverse[0], preferred_element_type=jnp.float32
    ).astype(jnp.bfloat16)
    col_targets = dev_index * cols_dev + jnp.arange(cols_dev, dtype=jnp.int32)
    whole_rows = lax.all_gather(lower_rows, "dev", axis=0, tiled=True)
    col_from = lax.dynamic_slice_in_dim(row_from, dev_index * cols_dev, cols_dev, 0)
    col_has = lax.dynamic_slice_in_dim(row_has, dev_index * cols_dev, cols_dev, 0)
    half_blocks = cols_dev // 2
    half = half_blocks * BLK
    front = parent_front.astype(jnp.float32)
    assembled_halves = []
    for part in range(2):
        cut = slice(part * half_blocks, (part + 1) * half_blocks)
        spread = placed_product(whole_rows, row_from, row_has, col_from[cut], col_has[cut])
        summed = lax.psum_scatter(spread, "sec", scatter_dimension=0, tiled=True)
        assembled_halves.append(
            front[:, part * half:(part + 1) * half] + summed.astype(jnp.float32)
        )
    pivot_blocks = parent_pivots.shape[0]
    pick_pivots = (parent_pivots[None, :] == col_targets[:, None]).astype(jnp.bfloat16)
    selected = jnp.einsum(
        "mr,rbk->mbk",
        pick_pivots,
        parent_inverse.reshape(pivot_blocks, BLK, -1),
        preferred_element_type=jnp.float32,
    ).astype(jnp.bfloat16)
    selected = selected.reshape(col_width, -1)
    order = selected.shape[1] // 2
    my_blocks = sec_index * rows_sec + jnp.arange(rows_sec, dtype=jnp.int32)
    is_pivot = jnp.any(parent_pivots[None, :] == my_blocks[:, None], axis=1)
    row_pivot = jnp.repeat(is_pivot, BLK)
    offset = dev_index * cols_dev % rows_sec * BLK
    roots = [dev * cols_dev // rows_sec for dev in range(dev_count)]
    relative = sec_index ^ (dev_index * cols_dev // rows_sec)
    bits = [1 << k for k in range((sec_count - 1).bit_length())]
    factor_halves, trailing_halves, column_starts = [], [], []
    for part in range(2):
        chosen = selected[:, part * order:(part + 1) * order]
        partial_sum = sum(
            jnp.dot(
                values.astype(jnp.bfloat16),
                chosen[index * half:(index + 1) * half],
                preferred_element_type=jnp.float32,
            )
            for index, values in enumerate(assembled_halves)
        )
        partial_sum = partial_sum.astype(jnp.bfloat16)
        if factor_halves:
            partial_sum, column_starts[-1] = lax.optimization_barrier(
                (partial_sum, column_starts[-1])
            )
        factor = lax.psum(partial_sum, "dev")
        trailing = jnp.where(row_pivot[:, None], jnp.zeros_like(factor), factor)
        factor_halves.append(factor)
        trailing_halves.append(trailing)
        column_starts.append(lax.dynamic_slice_in_dim(trailing, offset, col_width, 0))
    parent_factor = jnp.concatenate(factor_halves, axis=1)
    column_halves = [
        jnp.concatenate(
            [
                broadcast_rows(rows[:half], bits, dev_count, sec_count, roots, relative),
                broadcast_rows(rows[half:], bits[::-1], dev_count, sec_count, roots, relative),
            ],
            axis=0,
        )
        for rows in column_starts
    ]
    assembled = jnp.concatenate(assembled_halves, axis=1)
    parent_update = assembled - outer_rows(
        jnp.concatenate(trailing_halves, axis=1), jnp.concatenate(column_halves, axis=1)
    )
    return (parent_update, parent_factor)


def solution(mesh):
    placed = (P("sec", "dev", None), P("sec", None, None), P(), P("sec", "dev"), P(), P())
    return jax.shard_map(
        local,
        mesh=mesh,
        in_specs=placed,
        out_specs=(P("sec", "dev"), P("sec", None)),
        check_vma=False,
    )
```

```python
import jax
import jax.numpy as jnp
from jax import lax
from jax.experimental import pallas as pl
from jax.experimental.pallas import tpu as pltpu
from jax.sharding import PartitionSpec as P

BLK = 128
PORD = 8192


GROUP = 4


def broadcast_rows(value, bits, devs, dev_count, roots, relative):
    reached = [0]
    for bit in bits:
        pairs = [
            ((roots[dev] ^ rel) * dev_count + dev, (roots[dev] ^ rel ^ bit) * dev_count + dev)
            for dev in devs
            for rel in reached
        ]
        received = lax.ppermute(value, ("sec", "dev"), pairs)
        value = jnp.where((relative & bit) != 0, received, value)
        reached = reached + [rel ^ bit for rel in reached]
    return value


def scatter_sum(value, bits, sec_count, sec_index):
    digits = (sec_count - 1).bit_length()
    left = list(range(digits))[::-1]
    value = value.reshape((2,) * digits + value.shape[-2:])
    for bit in bits:
        place = bit.bit_length() - 1
        axis = left.index(place)
        mine = (sec_index >> place) & 1
        sent = lax.dynamic_index_in_dim(value, 1 - mine, axis, keepdims=False)
        kept = lax.dynamic_index_in_dim(value, mine, axis, keepdims=False)
        left.remove(place)
        received = lax.ppermute(sent, "sec", [(sec, sec ^ bit) for sec in range(sec_count)])
        value = kept.astype(jnp.float32) + received.astype(jnp.float32)
        if left:
            value = value.astype(jnp.bfloat16)
    return value


def placed_product(whole_rows, row_from, row_has, col_from, col_has):
    depth = whole_rows.shape[1]
    rows, cols = row_from.shape[0], col_from.shape[0]

    def kernel(row_from, row_has, col_from, col_has, *refs):
        left, right = refs[:GROUP], refs[GROUP:GROUP + cols]
        out, held = refs[GROUP + cols], refs[GROUP + cols + 1]
        step = pl.program_id(0)

        @pl.when(step == 0)
        def _():
            for k in range(cols):

                @pl.when(col_has[k] > 0)
                def _():
                    held[k * BLK:(k + 1) * BLK, :] = right[k][...]

                @pl.when(col_has[k] == 0)
                def _():
                    held[k * BLK:(k + 1) * BLK, :] = jnp.zeros((BLK, depth), held.dtype)

        product = outer_rows(jnp.concatenate([r[...] for r in left], axis=0), held[...])
        for k in range(GROUP):
            part = product[k * BLK:(k + 1) * BLK, :]
            kept = jnp.where(row_has[step * GROUP + k] > 0, -part, 0.0)
            out[k * BLK:(k + 1) * BLK, :] = kept.astype(out.dtype)

    def left_spec(k):
        return pl.BlockSpec((BLK, depth), lambda i, rf, rh, cf, ch: (rf[i * GROUP + k], 0))

    def right_spec(k):
        return pl.BlockSpec((BLK, depth), lambda i, rf, rh, cf, ch: (cf[k], 0))

    return pl.pallas_call(
        kernel,
        out_shape=jax.ShapeDtypeStruct((rows * BLK, cols * BLK), jnp.bfloat16),
        grid_spec=pltpu.PrefetchScalarGridSpec(
            num_scalar_prefetch=4,
            grid=(rows // GROUP,),
            in_specs=[left_spec(k) for k in range(GROUP)] + [right_spec(k) for k in range(cols)],
            out_specs=pl.BlockSpec((GROUP * BLK, cols * BLK), lambda i, rf, rh, cf, ch: (i, 0)),
            scratch_shapes=[pltpu.VMEM((cols * BLK, depth), jnp.bfloat16)],
        ),
        cost_estimate=pl.CostEstimate(
            flops=2 * rows * BLK * cols * BLK * depth,
            bytes_accessed=2 * rows * BLK * (depth + cols * BLK),
            transcendentals=0,
        ),
    )(row_from, row_has, col_from, col_has, *([whole_rows] * (GROUP + cols)))


def outer_rows(left_rows, right_rows):
    return lax.dot_general(
        left_rows, right_rows, (((1,), (1,)), ((), ())), preferred_element_type=jnp.float32
    )


def local(child_panel, child_inverse, child_map, parent_front, parent_inverse, parent_pivots):
    dev_count = lax.axis_size("dev")
    sec_count = lax.axis_size("sec")
    sec_index = lax.axis_index("sec")
    dev_index = lax.axis_index("dev")
    block_count = PORD // BLK
    cols_dev = block_count // dev_count
    rows_sec = block_count // sec_count
    col_width = cols_dev * BLK
    my_map = lax.dynamic_index_in_dim(child_map, sec_index, 0, keepdims=False)
    is_target = my_map[None, :] == jnp.arange(block_count, dtype=jnp.int32)[:, None]
    row_from = jnp.argmax(is_target, axis=1).astype(jnp.int32)
    row_has = jnp.any(is_target, axis=1).astype(jnp.int32)
    lower_rows = jnp.dot(
        child_panel[0], child_inverse[0], preferred_element_type=jnp.float32
    ).astype(jnp.bfloat16)
    col_targets = dev_index * cols_dev + jnp.arange(cols_dev, dtype=jnp.int32)
    whole_rows = lax.all_gather(lower_rows, "dev", axis=0, tiled=True)
    col_from = lax.dynamic_slice_in_dim(row_from, dev_index * cols_dev, cols_dev, 0)
    col_has = lax.dynamic_slice_in_dim(row_has, dev_index * cols_dev, cols_dev, 0)
    parts = dev_count // sec_count
    bits = [1 << k for k in range((sec_count - 1).bit_length())]
    half = col_width // 2
    row_from = row_from.reshape(sec_count, parts, -1)
    row_has = row_has.reshape(sec_count, parts, -1)
    assembled_parts = []
    for part in range(parts):
        spread = placed_product(
            whole_rows, row_from[:, part].reshape(-1), row_has[:, part].reshape(-1), col_from, col_has
        ).reshape(sec_count, -1, col_width)
        summed = jnp.concatenate(
            [
                scatter_sum(spread[:, :, :half], bits, sec_count, sec_index),
                scatter_sum(spread[:, :, half:], bits[::-1], sec_count, sec_index),
            ],
            axis=1,
        )
        front = parent_front[part * col_width:(part + 1) * col_width].astype(jnp.float32)
        assembled_parts.append(front + summed)
    pivot_blocks = parent_pivots.shape[0]
    pick_pivots = (parent_pivots[None, :] == col_targets[:, None]).astype(jnp.bfloat16)
    selected = jnp.einsum(
        "mr,rbk->mbk",
        pick_pivots,
        parent_inverse.reshape(pivot_blocks, BLK, -1),
        preferred_element_type=jnp.float32,
    ).astype(jnp.bfloat16)
    selected = selected.reshape(col_width, -1)
    my_blocks = sec_index * rows_sec + jnp.arange(rows_sec, dtype=jnp.int32)
    is_pivot = jnp.any(parent_pivots[None, :] == my_blocks[:, None], axis=1)
    row_pivot = jnp.repeat(is_pivot, BLK)
    roots = [dev * cols_dev // rows_sec for dev in range(dev_count)]
    relative = sec_index ^ (dev_index * cols_dev // rows_sec)
    factors, trailings = [], []
    for part in range(parts):
        partial_sum = jnp.dot(
            assembled_parts[part].astype(jnp.bfloat16), selected, preferred_element_type=jnp.float32
        ).astype(jnp.bfloat16)
        if part:
            partial_sum, trailings[-1] = lax.optimization_barrier((partial_sum, trailings[-1]))
        factor = lax.psum(partial_sum, "dev")
        masked = row_pivot[part * col_width:(part + 1) * col_width, None]
        factors.append(factor)
        trailings.append(jnp.where(masked, jnp.zeros_like(factor), factor))
    pieces = []
    for rows, order in ((slice(0, half), bits), (slice(half, None), bits[::-1])):
        piece = 0
        for part in range(parts):
            devs = range(part, dev_count, parts)
            moved = broadcast_rows(trailings[part][rows], order, devs, dev_count, roots, relative)
            piece = moved if part == 0 else jnp.where(dev_index % parts == part, moved, piece)
        pieces.append(piece)
    column_factor = jnp.concatenate(pieces, axis=0)
    parent_update = jnp.concatenate(
        [
            assembled - outer_rows(trailing, column_factor)
            for assembled, trailing in zip(assembled_parts, trailings)
        ],
        axis=0,
    )
    return (parent_update, jnp.concatenate(factors, axis=0))


def solution(mesh):
    placed = (P("sec", "dev", None), P("sec", None, None), P(), P("sec", "dev"), P(), P())
    return jax.shard_map(
        local,
        mesh=mesh,
        in_specs=placed,
        out_specs=(P("sec", "dev"), P("sec", None)),
        check_vma=False,
    )
```
